256 devices in a mesh: mem: 16 (over z, core), lat: 16 (over y, x).
Axes of the slice: x: 4, y: 4, z: 8, core: 2. Of those that a mesh axis runs over, the one named last changes fastest.
Arguments:
- state: bfloat16 [64, 12, 256, 2048], P('mem', None, 'lat'), may hold values from -6 to 6
- obs_cell: int32 [16, 16, 16384], P('lat', 'mem'), may hold values from 0 to 2047
- obs_value: float32 [16, 16, 16384], P('lat', 'mem'), may hold values from -6 to 6
- obs_rinv: float32 [16, 16, 16384], P('lat', 'mem'), may hold values from 0.005 to 0.1
- obs_count: int32 [16, 16], P('lat', 'mem'), may hold values from 1 to 16384, as said below
- loc_blocks: int32 [16, 16, 9], P('lat', 'mem'), may hold values 0 or 1
- chan_weight: float32 [12], replicated, may hold values from -1.75 to 1.75
Outputs:
- analysis: bfloat16 [64, 12, 256, 2048], P('mem', None, 'lat')
The draws below stay inside these ranges and needn't reach their ends.
Inputs may be any that keep to these rules, and one draw needn't show every extreme that they name: `obs_count`: some region has exactly 16384 live slots.
All inputs are finite; a program needn't handle non-finite values. No bound on the sum of `loc_blocks` on one device may be relied on, other than what follows from the above.
Results may differ from the reference program's by a relative error of at most 0.007.
Values may be sent and summed in bfloat16 or wider, within the bound.
A program may use at most 64 MiB of HBM per device.

```python
import math
import jax
import jax.numpy as jnp
from jax import lax

K = 64
C = 12
REG_LAT = 16
REG_LON = 128
CAP = 16384
NS_ITERS = 5
NRLAT = 16
NRLON = 16
NLAT = 256
NLON = 2048


def draw_obs_count(key, part):
    first, second, third = jax.random.split(key, 3)
    shape_all = (NRLAT, NRLON)
    halving = jax.random.randint(first, shape_all, 0, 4)
    base_count = CAP // jnp.power(2, halving)
    taken = jax.random.randint(second, shape_all, 0, 1 << 20) % (base_count // 2 + 1)
    counts = jnp.maximum(base_count - taken, 1).reshape(-1)
    chosen = jax.random.randint(third, (), 0, NRLAT * NRLON)
    counts = jnp.where(jnp.arange(NRLAT * NRLON) == chosen, CAP, counts)
    return counts.reshape(shape_all).astype(jnp.int32)


def draw_state(key, part):
    scale_key, noise_key = jax.random.split(jax.random.fold_in(key, 7), 2)
    log_scale = jax.random.uniform(scale_key, (K,), jnp.float32, math.log(0.25), 0.0)
    member_scale = jnp.exp(log_scale)[:, None, None, None]
    noise = jax.random.truncated_normal(noise_key, -6.0, 6.0, (K, C, NLAT, NLON), jnp.float32)
    values = member_scale * noise
    return values.astype(jnp.bfloat16)


def with_ends(entries, own_key, least, largest):
    dims = entries.shape
    spot = [jax.random.randint(jax.random.fold_in(own_key, axis), (), 0, dims[axis]) for axis in range(len(dims))]
    entries = entries.at[tuple(spot)].set(least)
    longest = dims.index(max(dims))
    spot[longest] = (spot[longest] + 1) % dims[longest]
    return entries.at[tuple(spot)].set(largest)


def block_levels(own_key, extent, shards, smallest, high):
    gain, own = 1.0, jax.random.fold_in(own_key, 6)
    for axis_at, blocks in shards:
        draws = jnp.exp(jax.random.uniform(jax.random.fold_in(own, axis_at), (blocks,), jnp.float32, smallest / len(shards), high / len(shards)))
        gain = gain * jnp.repeat(draws, extent[axis_at] // blocks).reshape([-1 if axis == axis_at else 1 for axis in range(len(extent))])
    return gain


def centred(stream_key, dims, scale, bound, cuts=(), kind=jnp.bfloat16):
    drawn = jax.random.normal(stream_key, dims, jnp.float32) * scale
    if len(cuts) > 0:
        drawn = block_levels(stream_key, dims, cuts, -0.22, 0.18) * drawn
    return jnp.clip(drawn, min=-bound, max=bound).astype(kind)


def setup_inputs(seed: int = 0) -> dict:
    keys = jax.random.split(jax.random.key(seed), 8)
    state = draw_state(jax.random.fold_in(keys[7], 71), 0)
    obs_cell = with_ends(jax.random.randint(keys[1], (NRLAT, NRLON, CAP), 0, REG_LAT * REG_LON), jax.random.fold_in(keys[1], 1), 0, (REG_LAT * REG_LON) - 1).astype(jnp.int32)
    obs_value = centred(keys[2], (NRLAT, NRLON, CAP), 1.0, 6.0, ((0, 16), (1, 16)), jnp.float32)
    obs_rinv = jnp.clip(jnp.exp(math.log(0.1) - 2.9957323 * jax.random.uniform(keys[3], (NRLAT, NRLON, CAP), jnp.float32) ** block_levels(keys[3], (NRLAT, NRLON, CAP), ((0, 16), (1, 16)), -0.2, 0.2)), 0.005, 0.1)
    obs_count = draw_obs_count(jax.random.fold_in(keys[7], 71), 0)
    loc_blocks = with_ends((jax.random.randint(keys[5], (NRLAT, NRLON, 9), 0, 4) < 3).astype(jnp.int32), jax.random.fold_in(keys[5], 1), 0, 1)
    chan_weight = centred(keys[6], (C,), C ** -0.5, 1.75, (), jnp.float32)
    return dict(state=state, obs_cell=obs_cell, obs_value=obs_value, obs_rinv=obs_rinv, obs_count=obs_count, loc_blocks=loc_blocks, chan_weight=chan_weight)


def inverse_root(matrix):
    size_k = matrix.shape[-1]
    identity = jnp.eye(size_k, dtype=jnp.float32)
    frobenius = jnp.sqrt(lax.optimization_barrier(jnp.sum(matrix * matrix, axis=(-2, -1), keepdims=True)))
    current = matrix / frobenius
    inverse = jnp.broadcast_to(identity, matrix.shape)
    for sweep_index in range(NS_ITERS):
        middle = 0.5 * (3.0 * identity - jnp.matmul(inverse, current, precision=lax.Precision.HIGHEST))
        current = jnp.matmul(current, middle, precision=lax.Precision.HIGHEST)
        inverse = jnp.matmul(middle, inverse, precision=lax.Precision.HIGHEST)
    return inverse / jnp.sqrt(frobenius)

def weights_from(combined):
    members = combined.shape[-1] - 1
    gram_part = combined[:, :members, :members]
    across = combined[:, :members, members]
    system = (members - 1.0) * jnp.eye(members, dtype=jnp.float32) + gram_part
    root_matrix = inverse_root(system)
    half_step = jnp.einsum('rjk,rk->rj', root_matrix, across, precision=lax.Precision.HIGHEST)
    shift_mean = jnp.einsum('rjk,rk->rj', root_matrix, half_step, precision=lax.Precision.HIGHEST)
    return (jnp.sqrt(members - 1.0) * root_matrix + shift_mean[:, :, None]).astype(jnp.bfloat16)

def observe(region_tile, cell_ids, values, inverse_var, live_count, chan_weight):
    projected = jnp.einsum('kcyx,c->kyx', region_tile.astype(jnp.float32), chan_weight)
    flat_cells = projected.reshape(projected.shape[0], -1)
    values_at = jnp.take(flat_cells, cell_ids, axis=1)
    obs_mean = lax.optimization_barrier(jnp.mean(values_at, axis=0))
    live_slots = (jnp.arange(cell_ids.shape[0]) < live_count).astype(jnp.float32)
    obs_scale = jnp.sqrt(inverse_var) * live_slots
    obs_pert = (values_at - obs_mean) * obs_scale
    innovation = (values - obs_mean) * obs_scale
    return jnp.concatenate([obs_pert, innovation[None]], 0).astype(jnp.bfloat16)

def reference(state, obs_cell, obs_value, obs_rinv, obs_count, loc_blocks, chan_weight):
    tiles = state.reshape(K, C, NRLAT, REG_LAT, NRLON, REG_LON).transpose(2, 4, 0, 1, 3, 5)
    tiles = tiles.reshape(NRLAT * NRLON, K, C, REG_LAT, REG_LON)

    def block_product(inputs):
        region_tile, cell_ids, values, inverse_var, counts = inputs
        scaled_obs = observe(region_tile, cell_ids, values, inverse_var, counts, chan_weight)
        return jnp.dot(scaled_obs, scaled_obs.T, preferred_element_type=jnp.float32)
    block_grams = lax.map(block_product, (tiles, obs_cell.reshape(-1, CAP), obs_value.reshape(-1, CAP), obs_rinv.reshape(-1, CAP), obs_count.reshape(-1)))
    block_grams = block_grams.reshape(NRLAT, NRLON, K + 1, K + 1)
    wrapped = jnp.concatenate([block_grams[:, -1:], block_grams, block_grams[:, :1]], 1)
    padded = jnp.pad(wrapped, ((1, 1), (0, 0), (0, 0), (0, 0)))
    combined = jnp.zeros((NRLAT, NRLON, K + 1, K + 1), jnp.float32)
    for row_off in range(3):
        for col_off in range(3):
            factor = loc_blocks[:, :, 3 * row_off + col_off].astype(jnp.float32)[:, :, None, None]
            combined = combined + factor * padded[row_off:row_off + NRLAT, col_off:col_off + NRLON]
    transforms = weights_from(combined.reshape(-1, K + 1, K + 1))

    def analyse(inputs):
        region_tile, transform = inputs
        widened = region_tile.astype(jnp.float32)
        mean_tile = lax.optimization_barrier(jnp.mean(widened, axis=0))
        perts = lax.optimization_barrier((widened - mean_tile).astype(jnp.bfloat16))
        transform = lax.optimization_barrier(transform)
        shifted = jnp.einsum('jcyx,jk->kcyx', perts.astype(jnp.float32), transform.astype(jnp.float32))
        return (mean_tile + shifted).astype(jnp.bfloat16)
    analysis = lax.map(analyse, (tiles, transforms))
    analysis = analysis.reshape(NRLAT, NRLON, K, C, REG_LAT, REG_LON).transpose(2, 3, 0, 4, 1, 5)
    return analysis.reshape(K, C, NLAT, NLON)
```

```python
import functools

import jax
import jax.numpy as jnp
from jax import lax
from jax.experimental import pallas as pl
from jax.experimental.pallas import tpu as pltpu
from jax.sharding import PartitionSpec as P

NS_ITERS = 5
MESH = pl.DeviceIdType.MESH
HIGHEST = lax.Precision.HIGHEST
F32 = jnp.float32
BF16 = jnp.bfloat16


def peer(me, size, index):
    step = jnp.maximum(index - 1, 0)
    distance = step // 4 + 1
    offset = jnp.where((step // 2) % 2 == 0, distance, size // 2 - distance)
    offset = jnp.where(index == 0, 0, offset)
    flip = jnp.where(index == 0, 1, step % 2)
    return ((me // 2 + offset) % (size // 2)) * 2 + (me + flip) % 2


def kernel(
    weight, count, loc,
    x, cell, value, rinv,
    out,
    xv, cellv, valuev, rinvv, proj, projected, table, gram, gram_out, near, arrived, spread, weights, perts, means, analysed,
    load_sem, obs_sem, own_sem, proj_send, proj_recv, gram_send, gram_recv, in_send, in_recv, out_send, out_recv,
):
    n = lax.axis_size("mem")
    bands = lax.axis_size("lat")
    me, band = lax.axis_index("mem"), lax.axis_index("lat")
    per, channels, rows, width = x.shape
    members = per * n
    cols = width // n

    loads = [pltpu.make_async_copy(x.at[m], xv.at[m], load_sem.at[m]) for m in range(per)]
    for load in loads:
        load.start()
    obs_loads = [
        pltpu.make_async_copy(source, target, obs_sem.at[i])
        for i, (source, target) in enumerate(((cell, cellv), (value, valuev), (rinv, rinvv)))
    ]
    for load in obs_loads:
        load.start()

    def columns(q):
        return pl.ds(pl.multiple_of(q * cols, cols), cols)

    neighbours = [(i, j) for i in (-1, 0, 1) for j in (-1, 0, 1) if (i, j) != (0, 0)]

    def neighbour(i, j):
        return {"lat": (band + i + bands) % bands, "mem": (me + j + n) % n}

    barrier = pltpu.get_barrier_semaphore()

    def greet(i, carry):
        pl.semaphore_signal(barrier, inc=1, device_id={"mem": peer(me, n, i)}, device_id_type=MESH)
        return carry

    lax.fori_loop(0, n - 1, greet, 0)
    for i, j in neighbours:
        if i != 0:
            pl.semaphore_signal(barrier, inc=1, device_id=neighbour(i, j), device_id_type=MESH)

    wide = 256
    for m in range(per):
        loads[m].wait()

        def project(b, carry):
            at = pl.ds(pl.multiple_of(b * wide, wide), wide)
            total = xv[m, 0, :, at].astype(F32) * weight[0]
            for c in range(1, channels):
                total = total + xv[m, c, :, at].astype(F32) * weight[c]
            proj[m, :, at] = total.astype(BF16)
            return carry

        lax.fori_loop(0, width // wide, project, 0)

    pl.semaphore_wait(barrier, n - 1 + 6)

    mine = pl.ds(pl.multiple_of(me * per, per), per)

    def send_proj(i, carry):
        q = peer(me, n, i)
        pltpu.make_async_remote_copy(
            src_ref=proj.at[:, :, columns(q)],
            dst_ref=projected.at[mine],
            send_sem=proj_send, recv_sem=proj_recv,
            device_id={"mem": q}, device_id_type=MESH,
        ).start()
        return carry

    lax.fori_loop(0, n - 1, send_proj, 0)

    def send_in(c):
        def one(i, carry):
            q = peer(me, n, i)
            pltpu.make_async_remote_copy(
                src_ref=x.at[:, pl.ds(c, 1), :, columns(q)],
                dst_ref=arrived.at[mine, pl.ds(c, 1)],
                send_sem=in_send.at[c], recv_sem=in_recv.at[c],
                device_id={"mem": q}, device_id_type=MESH,
            ).start()
            return carry

        lax.fori_loop(0, n - 1, one, 0)

    def drain(ref, sem):
        pltpu.make_async_copy(ref, ref, sem).wait()

    others = pl.ds(0, members - per)

    def next_in(c):
        drain(arrived.at[others, pl.ds(c - 2, 1)], in_send.at[c - 2])
        send_in(c)

    own_proj = pltpu.make_async_copy(proj.at[:, :, columns(me)], projected.at[mine], own_sem.at[0])
    own_in = pltpu.make_async_copy(x.at[:, :, :, columns(me)], arrived.at[mine], own_sem.at[1])
    own_proj.start()
    own_in.start()
    send_in(0)
    send_in(1)

    for_member = lax.broadcasted_iota(jnp.int32, (members, members * rows), 0)
    spread[...] = jnp.where(
        for_member == lax.broadcasted_iota(jnp.int32, (members, members * rows), 1) // rows, 1.0, 0.0
    ).astype(BF16)

    for load in obs_loads:
        load.wait()
    block = 8
    lanes = cellv.shape[1]
    row_of = lax.broadcasted_iota(jnp.int32, (rows, block * lanes), 0)
    col_of = lax.broadcasted_iota(jnp.int32, (cols, block * lanes), 0)

    def along(tile):
        return jnp.concatenate([tile[i : i + 1, :] for i in range(block)], axis=1)

    def histogram(b, total):
        at = pl.ds(pl.multiple_of(b * block, block), block)
        slot = (
            b * (block * lanes)
            + lax.broadcasted_iota(jnp.int32, (block, lanes), 0) * lanes
            + lax.broadcasted_iota(jnp.int32, (block, lanes), 1)
        )
        live = jnp.where(slot < count[0, 0], rinvv[at, :], 0.0)
        held = live * valuev[at, :]
        cells = along(cellv[at, :])
        hit = row_of == cells // cols
        parts = []
        for term in (live, held):
            high = term.astype(BF16).astype(F32)
            parts += [high, term - high]
        terms = jnp.concatenate([jnp.where(hit, along(part), 0.0) for part in parts], axis=0).astype(BF16)
        onehot = jnp.where(col_of == cells % cols, 1.0, 0.0).astype(BF16)
        return total + lax.dot_general(terms, onehot, (((1,), (1,)), ((), ())), preferred_element_type=F32)

    sums = lax.fori_loop(0, cellv.shape[0] // block, histogram, jnp.zeros((4 * rows, cols), F32))
    cell_rinv = sums[:rows] + sums[rows : 2 * rows]
    cell_held = sums[2 * rows : 3 * rows] + sums[3 * rows :]
    next_in(2)

    own_proj.wait()
    drain(projected.at[others], proj_recv)
    step = 8
    total = jnp.zeros((rows, cols), F32)
    for k in range(0, members, step):
        total = total + jnp.sum(projected[k : k + step].astype(F32), axis=0)
    obs_mean = total * (1.0 / members)
    seen = cell_rinv > 0.0
    root_rinv = jnp.sqrt(cell_rinv)
    inverse = jnp.where(seen, 1.0 / jnp.where(seen, root_rinv, 1.0), 0.0)
    for k in range(0, members, step):
        table[k : k + step] = (projected[k : k + step].astype(F32) - obs_mean[None]) * root_rinv[None]
    tail = table.shape[0] - members
    table[members:] = jnp.zeros((tail, rows, cols), F32)
    table[members] = (cell_held - cell_rinv * obs_mean) * inverse
    lines = jnp.concatenate([table[:, r, :].astype(BF16) for r in range(rows)], axis=1)
    gram[...] = lax.dot_general(lines[:members], lines, (((1,), (1,)), ((), ())), preferred_element_type=F32)
    gram_out[...] = gram[...].astype(BF16)
    next_in(3)

    for s, (i, j) in enumerate(neighbours):
        pltpu.make_async_remote_copy(
            src_ref=gram_out, dst_ref=near.at[7 - s],
            send_sem=gram_send, recv_sem=gram_recv,
            device_id=neighbour(i, j), device_id_type=MESH,
        ).start()
    next_in(4)
    next_in(5)
    drain(near, gram_recv)
    combined = gram[...] * loc[0, 4].astype(F32)
    for s, (i, j) in enumerate(neighbours):
        factor = loc[0, 3 * (i + 1) + (j + 1)]
        if i == -1:
            factor = jnp.where(band > 0, factor, 0)
        if i == 1:
            factor = jnp.where(band < bands - 1, factor, 0)
        combined = combined + factor.astype(F32) * near[s].astype(F32)

    identity = jnp.where(
        lax.broadcasted_iota(jnp.int32, (members, members), 0)
        == lax.broadcasted_iota(jnp.int32, (members, members), 1),
        1.0, 0.0,
    )

    def times(a, b):
        return jnp.dot(a, b, precision=HIGHEST, preferred_element_type=F32)

    system = (members - 1.0) * identity + combined[:, :members]
    across = combined[:, members : members + 1]
    frobenius = jnp.sqrt(jnp.sum(jnp.sum(system * system, axis=1, keepdims=True), axis=0, keepdims=True))
    current = system / frobenius

    inverse = identity
    for _ in range(NS_ITERS):
        middle = 0.5 * (3.0 * identity - times(inverse, current))
        current, inverse = times(current, middle), times(middle, inverse)
    root = inverse / jnp.sqrt(frobenius)
    half = jnp.sum(root * across, axis=0, keepdims=True)
    half = jnp.sum(identity * half, axis=1, keepdims=True)
    shift = jnp.sum(root * half, axis=0, keepdims=True)
    transform = (float(members - 1) ** 0.5 * root + shift).astype(BF16)
    next_in(6)

    tall = 128
    repeated = jnp.dot(transform, spread[...], preferred_element_type=F32).astype(BF16)

    def expand(b, carry):
        at = lax.broadcasted_iota(jnp.int32, (tall, members), 0) + b * tall
        pick = jnp.where(
            at // rows == lax.broadcasted_iota(jnp.int32, (tall, members), 1), 1.0, 0.0
        ).astype(BF16)
        full = jnp.dot(pick, repeated, preferred_element_type=F32)
        same = (
            lax.broadcasted_iota(jnp.int32, full.shape, 0) % rows
            == lax.broadcasted_iota(jnp.int32, full.shape, 1) % rows
        )
        weights[pl.ds(pl.multiple_of(b * tall, tall), tall), :] = jnp.where(same, full, 0.0).astype(BF16)
        return carry

    lax.fori_loop(0, members * rows // tall, expand, 0)
    lax.fori_loop(7, channels, lambda c, carry: (next_in(c), carry)[1], 0)
    own_in.wait()

    high = 256

    def analyse(p, carry):
        for h in range(2):
            c = 2 * p + h
            drain(arrived.at[others, pl.ds(c, 1)], in_recv.at[c])
            total = jnp.zeros((rows, cols), F32)
            for k in range(0, members, step):
                total = total + jnp.sum(arrived[k : k + step, c].astype(F32), axis=0)
            mean = total * (1.0 / members)
            means[h] = mean
            for k in range(0, members, step):
                part = (arrived[k : k + step, c].astype(F32) - mean[None]).astype(BF16)
                perts[k * rows : (k + step) * rows, h * cols : (h + 1) * cols] = part.reshape(step * rows, cols)

        def mix(b, inner):
            at = pl.ds(pl.multiple_of(b * high, high), high)
            shifted = jnp.dot(weights[at, :], perts[...], preferred_element_type=F32)
            for h in range(2):
                part = shifted[:, h * cols : (h + 1) * cols].reshape(high // rows, rows, cols) + means[h][None]
                analysed[pl.ds(b * (high // rows), high // rows), 2 * p + h] = part.astype(BF16)
            return inner

        lax.fori_loop(0, members * rows // high, mix, 0)

        def one(i, inner):
            q = peer(me, n, i)
            pltpu.make_async_remote_copy(
                src_ref=analysed.at[pl.ds(q * per, per), pl.ds(2 * p, 2)],
                dst_ref=out.at[:, pl.ds(2 * p, 2), :, columns(me)],
                send_sem=out_send, recv_sem=out_recv,
                device_id={"mem": q}, device_id_type=MESH,
            ).start()
            return inner

        lax.fori_loop(0, n - 1, one, 0)
        return carry

    lax.fori_loop(0, channels // 2, analyse, 0)
    own_out = pltpu.make_async_copy(analysed.at[mine], out.at[:, :, :, columns(me)], own_sem.at[2])
    own_out.start()

    drain(projected.at[others], proj_send)
    drain(near, gram_send)
    for c in (channels - 2, channels - 1):
        drain(arrived.at[others, pl.ds(c, 1)], in_send.at[c])
    own_out.wait()
    drain(analysed.at[others], out_send)
    drain(analysed.at[others], out_recv)


def shards(state, obs_cell, obs_value, obs_rinv, obs_count, loc_blocks, chan_weight):
    per, channels, rows, width = state.shape
    n = lax.axis_size("mem")
    members, cols = per * n, width // n
    slots = obs_cell.shape[2]
    lanes = 128
    obs_shape = (slots // lanes, lanes)
    whole = pl.BlockSpec(memory_space=pl.ANY)
    scalars = pl.BlockSpec(memory_space=pltpu.SMEM)
    dma = pltpu.SemaphoreType.DMA
    return pl.pallas_call(
        kernel,
        out_shape=jax.ShapeDtypeStruct(state.shape, BF16),
        in_specs=[scalars] * 3 + [whole] * 4,
        out_specs=whole,
        scratch_shapes=[
            pltpu.VMEM(state.shape, BF16),
            pltpu.VMEM(obs_shape, jnp.int32),
            pltpu.VMEM(obs_shape, F32),
            pltpu.VMEM(obs_shape, F32),
            pltpu.VMEM((per, rows, width), BF16),
            pltpu.VMEM((members, rows, cols), BF16),
            pltpu.VMEM((128, rows, cols), F32),
            pltpu.VMEM((members, 128), F32),
            pltpu.VMEM((members, 128), BF16),
            pltpu.VMEM((8, members, 128), BF16),
            pltpu.VMEM((members, channels, rows, cols), BF16),
            pltpu.VMEM((members, members * rows), BF16),
            pltpu.VMEM((members * rows, members * rows), BF16),
            pltpu.VMEM((members * rows, 2 * cols), BF16),
            pltpu.VMEM((2, rows, cols), F32),
            pltpu.VMEM((members, channels, rows, cols), BF16),
            dma((per,)),
            dma((3,)),
            dma((3,)),
            dma, dma, dma, dma,
            dma((channels,)),
            dma((channels,)),
            dma, dma,
        ],
        compiler_params=pltpu.CompilerParams(
            collective_id=0, has_side_effects=True, vmem_limit_bytes=56 * 2**20
        ),
        name="letkf",
    )(
        chan_weight, obs_count, loc_blocks[0],
        state, obs_cell.reshape(obs_shape), obs_value.reshape(obs_shape), obs_rinv.reshape(obs_shape),
    )


def solution(mesh):
    placed = (
        P("mem", None, "lat", None),
        P("lat", "mem", None),
        P("lat", "mem", None),
        P("lat", "mem", None),
        P("lat", "mem"),
        P("lat", "mem", None),
        P(),
    )
    return jax.shard_map(
        shards, mesh=mesh, in_specs=placed, out_specs=P("mem", None, "lat", None), check_vma=False
    )
```

```python
import functools

import jax
import jax.numpy as jnp
from jax import lax
from jax.experimental import pallas as pl
from jax.experimental.pallas import tpu as pltpu
from jax.sharding import PartitionSpec as P

NS_ITERS = 5
MESH = pl.DeviceIdType.MESH
HIGHEST = lax.Precision.HIGHEST
F32 = jnp.float32
BF16 = jnp.bfloat16


def peer(me, size, index):
    step = jnp.maximum(index - 1, 0)
    distance = step // 4 + 1
    offset = jnp.where((step // 2) % 2 == 0, distance, size // 2 - distance)
    offset = jnp.where(index == 0, 0, offset)
    flip = jnp.where(index == 0, 1, step % 2)
    return ((me // 2 + offset) % (size // 2)) * 2 + (me + flip) % 2


def basis(weight):
    channels = weight.shape[0]
    big = 2.0**60
    total = (weight[0] * big) * (weight[0] * big)
    for c in range(1, channels):
        total = total + (weight[c] * big) * (weight[c] * big)
    norm = jnp.sqrt(jnp.full((8, 128), total, F32))
    some = norm > 0.0
    inverse = jnp.where(some, 1.0 / jnp.where(some, norm, 1.0), 0.0)
    first = jnp.where(some, jnp.abs(weight[0]) * big * inverse, 1.0)
    sign = jnp.where(weight[0] < 0.0, -1.0, 1.0)
    a, g = jnp.max(first), jnp.max(1.0 / (1.0 + first))
    return a, jnp.max(inverse) * big * sign, g, jnp.max(norm) * (1.0 / big) * sign


def kernel(
    weight, count, loc,
    x, cell, value, rinv,
    out,
    xv, cellv, valuev, rinvv, shared, table, gram, gram_out, near, arrived, spread, weights, perts, means, analysed,
    load_sem, obs_sem, own_sem, gram_send, gram_recv, in_send, in_recv, out_send, out_recv,
):
    n = lax.axis_size("mem")
    bands = lax.axis_size("lat")
    me, band = lax.axis_index("mem"), lax.axis_index("lat")
    per, channels, rows, width = x.shape
    members = per * n
    cols = width // n

    loads = [pltpu.make_async_copy(x.at[m], xv.at[m], load_sem.at[m]) for m in range(per)]
    for load in loads:
        load.start()
    obs_loads = [
        pltpu.make_async_copy(source, target, obs_sem.at[i])
        for i, (source, target) in enumerate(((cell, cellv), (value, valuev), (rinv, rinvv)))
    ]
    for load in obs_loads:
        load.start()

    def columns(q):
        return pl.ds(pl.multiple_of(q * cols, cols), cols)

    neighbours = [(i, j) for i in (-1, 0, 1) for j in (-1, 0, 1) if (i, j) != (0, 0)]

    def neighbour(i, j):
        return {"lat": (band + i + bands) % bands, "mem": (me + j + n) % n}

    barrier = pltpu.get_barrier_semaphore()

    def greet(i, carry):
        pl.semaphore_signal(barrier, inc=1, device_id={"mem": peer(me, n, i)}, device_id_type=MESH)
        return carry

    lax.fori_loop(0, n - 1, greet, 0)
    for i, j in neighbours:
        if i != 0:
            pl.semaphore_signal(barrier, inc=1, device_id=neighbour(i, j), device_id_type=MESH)

    a, per_weight, g, to_observed = basis(weight)
    wide = 256
    for m in range(per):
        loads[m].wait()

        def first_channel(b, carry):
            at = pl.ds(pl.multiple_of(b * wide, wide), wide)
            x0 = xv[m, 0, :, at].astype(F32)
            total = x0 * a
            for c in range(1, channels):
                total = total + xv[m, c, :, at].astype(F32) * (weight[c] * per_weight)
            xv[m, 0, :, at] = total.astype(BF16)
            shared[m, :, at] = total + x0
            return carry

        lax.fori_loop(0, width // wide, first_channel, 0)

    def other_channel(c):
        factor = weight[c] * per_weight * g

        def one(b, carry):
            at = pl.ds(pl.multiple_of(b * wide, wide), wide)
            for m in range(per):
                xv[m, c, :, at] = (xv[m, c, :, at].astype(F32) - shared[m, :, at] * factor).astype(BF16)
            return carry

        lax.fori_loop(0, width // wide, one, 0)

    pl.semaphore_wait(barrier, n - 1 + 6)

    mine = pl.ds(pl.multiple_of(me * per, per), per)

    def send_in(c):
        def one(i, carry):
            q = peer(me, n, i)
            pltpu.make_async_remote_copy(
                src_ref=xv.at[:, pl.ds(c, 1), :, columns(q)],
                dst_ref=arrived.at[mine, pl.ds(c, 1)],
                send_sem=in_send.at[c], recv_sem=in_recv.at[c],
                device_id={"mem": q}, device_id_type=MESH,
            ).start()
            return carry

        lax.fori_loop(0, n - 1, one, 0)

    def drain(ref, sem):
        pltpu.make_async_copy(ref, ref, sem).wait()

    others = pl.ds(0, members - per)

    def next_in(c):
        drain(arrived.at[others, pl.ds(c - 3, 1)], in_send.at[c - 3])
        send_in(c)

    def own_in(start, size, i):
        return pltpu.make_async_copy(
            xv.at[:, pl.ds(start, size), :, columns(me)], arrived.at[mine, pl.ds(start, size)], own_sem.at[i]
        )

    send_in(0)
    own_in(0, 1, 0).start()
    for c in (1, 2):
        other_channel(c)
        send_in(c)
    lax.fori_loop(3, channels, lambda c, carry: (other_channel(c), carry)[1], 0)
    own_in(1, channels - 1, 1).start()

    for_member = lax.broadcasted_iota(jnp.int32, (members, members * rows), 0)
    spread[...] = jnp.where(
        for_member == lax.broadcasted_iota(jnp.int32, (members, members * rows), 1) // rows, 1.0, 0.0
    ).astype(BF16)

    for load in obs_loads:
        load.wait()
    block = 8
    lanes = cellv.shape[1]
    row_of = lax.broadcasted_iota(jnp.int32, (rows, block * lanes), 0)
    col_of = lax.broadcasted_iota(jnp.int32, (cols, block * lanes), 0)

    def along(tile):
        return jnp.concatenate([tile[i : i + 1, :] for i in range(block)], axis=1)

    def histogram(b, total):
        at = pl.ds(pl.multiple_of(b * block, block), block)
        slot = (
            b * (block * lanes)
            + lax.broadcasted_iota(jnp.int32, (block, lanes), 0) * lanes
            + lax.broadcasted_iota(jnp.int32, (block, lanes), 1)
        )
        live = jnp.where(slot < count[0, 0], rinvv[at, :], 0.0)
        held = live * valuev[at, :]
        cells = along(cellv[at, :])
        hit = row_of == cells // cols
        parts = []
        for term in (live, held):
            high = term.astype(BF16).astype(F32)
            parts += [high, term - high]
        terms = jnp.concatenate([jnp.where(hit, along(part), 0.0) for part in parts], axis=0).astype(BF16)
        onehot = jnp.where(col_of == cells % cols, 1.0, 0.0).astype(BF16)
        return total + lax.dot_general(terms, onehot, (((1,), (1,)), ((), ())), preferred_element_type=F32)

    sums = lax.fori_loop(0, cellv.shape[0] // block, histogram, jnp.zeros((4 * rows, cols), F32))
    cell_rinv = sums[:rows] + sums[rows : 2 * rows]
    cell_held = sums[2 * rows : 3 * rows] + sums[3 * rows :]
    next_in(3)

    own_in(0, 1, 0).wait()
    drain(arrived.at[others, pl.ds(0, 1)], in_recv.at[0])
    step = 8
    total = jnp.zeros((rows, cols), F32)
    for k in range(0, members, step):
        total = total + jnp.sum(arrived[k : k + step, 0].astype(F32), axis=0)
    obs_mean = total * (1.0 / members)
    seen = cell_rinv > 0.0
    root_rinv = jnp.sqrt(cell_rinv)
    inverse = jnp.where(seen, 1.0 / jnp.where(seen, root_rinv, 1.0), 0.0)
    scale = root_rinv * to_observed
    for k in range(0, members, step):
        table[k : k + step] = (arrived[k : k + step, 0].astype(F32) - obs_mean[None]) * scale[None]
    tail = table.shape[0] - members
    table[members:] = jnp.zeros((tail, rows, cols), F32)
    table[members] = (cell_held - cell_rinv * (obs_mean * to_observed)) * inverse
    lines = jnp.concatenate([table[:, r, :].astype(BF16) for r in range(rows)], axis=1)
    gram[...] = lax.dot_general(lines[:members], lines, (((1,), (1,)), ((), ())), preferred_element_type=F32)
    gram_out[...] = gram[...].astype(BF16)

    for s, (i, j) in enumerate(neighbours):
        pltpu.make_async_remote_copy(
            src_ref=gram_out, dst_ref=near.at[7 - s],
            send_sem=gram_send, recv_sem=gram_recv,
            device_id=neighbour(i, j), device_id_type=MESH,
        ).start()
    next_in(4)
    next_in(5)
    drain(near, gram_recv)
    combined = gram[...] * loc[0, 4].astype(F32)
    for s, (i, j) in enumerate(neighbours):
        factor = loc[0, 3 * (i + 1) + (j + 1)]
        if i == -1:
            factor = jnp.where(band > 0, factor, 0)
        if i == 1:
            factor = jnp.where(band < bands - 1, factor, 0)
        combined = combined + factor.astype(F32) * near[s].astype(F32)

    identity = jnp.where(
        lax.broadcasted_iota(jnp.int32, (members, members), 0)
        == lax.broadcasted_iota(jnp.int32, (members, members), 1),
        1.0, 0.0,
    )

    def times(a, b):
        return jnp.dot(a, b, precision=HIGHEST, preferred_element_type=F32)

    system = (members - 1.0) * identity + combined[:, :members]
    across = combined[:, members : members + 1]
    frobenius = jnp.sqrt(jnp.sum(jnp.sum(system * system, axis=1, keepdims=True), axis=0, keepdims=True))
    current = system / frobenius

    inverse = identity
    for _ in range(NS_ITERS):
        middle = 0.5 * (3.0 * identity - times(inverse, current))
        current, inverse = times(current, middle), times(middle, inverse)
    root = inverse / jnp.sqrt(frobenius)
    half = jnp.sum(root * across, axis=0, keepdims=True)
    half = jnp.sum(identity * half, axis=1, keepdims=True)
    shift = jnp.sum(root * half, axis=0, keepdims=True)
    transform = (float(members - 1) ** 0.5 * root + shift).astype(BF16)
    next_in(6)

    tall = 128
    repeated = jnp.dot(transform, spread[...], preferred_element_type=F32).astype(BF16)

    def expand(b, carry):
        at = lax.broadcasted_iota(jnp.int32, (tall, members), 0) + b * tall
        pick = jnp.where(
            at // rows == lax.broadcasted_iota(jnp.int32, (tall, members), 1), 1.0, 0.0
        ).astype(BF16)
        full = jnp.dot(pick, repeated, preferred_element_type=F32)
        same = (
            lax.broadcasted_iota(jnp.int32, full.shape, 0) % rows
            == lax.broadcasted_iota(jnp.int32, full.shape, 1) % rows
        )
        weights[pl.ds(pl.multiple_of(b * tall, tall), tall), :] = jnp.where(same, full, 0.0).astype(BF16)
        return carry

    lax.fori_loop(0, members * rows // tall, expand, 0)
    lax.fori_loop(7, channels, lambda c, carry: (next_in(c), carry)[1], 0)
    own_in(1, channels - 1, 1).wait()

    high = 256

    def analyse(p, carry):
        for h in range(2):
            c = 2 * p + h
            if h == 0:
                @pl.when(p > 0)
                def _():
                    drain(arrived.at[others, pl.ds(c, 1)], in_recv.at[c])
            else:
                drain(arrived.at[others, pl.ds(c, 1)], in_recv.at[c])
            total = jnp.zeros((rows, cols), F32)
            for k in range(0, members, step):
                total = total + jnp.sum(arrived[k : k + step, c].astype(F32), axis=0)
            mean = total * (1.0 / members)
            means[h] = mean
            for k in range(0, members, step):
                part = (arrived[k : k + step, c].astype(F32) - mean[None]).astype(BF16)
                perts[k * rows : (k + step) * rows, h * cols : (h + 1) * cols] = part.reshape(step * rows, cols)

        def mix(b, inner):
            at = pl.ds(pl.multiple_of(b * high, high), high)
            shifted = jnp.dot(weights[at, :], perts[...], preferred_element_type=F32)
            for h in range(2):
                part = shifted[:, h * cols : (h + 1) * cols].reshape(high // rows, rows, cols) + means[h][None]
                analysed[pl.ds(b * (high // rows), high // rows), 2 * p + h] = part.astype(BF16)
            return inner

        lax.fori_loop(0, members * rows // high, mix, 0)

        def one(i, inner):
            q = peer(me, n, i)
            pltpu.make_async_remote_copy(
                src_ref=analysed.at[pl.ds(q * per, per), pl.ds(2 * p, 2)],
                dst_ref=out.at[:, pl.ds(2 * p, 2), :, columns(me)],
                send_sem=out_send, recv_sem=out_recv,
                device_id={"mem": q}, device_id_type=MESH,
            ).start()
            return inner

        lax.fori_loop(0, n - 1, one, 0)
        return carry

    lax.fori_loop(0, channels // 2, analyse, 0)
    own_out = pltpu.make_async_copy(analysed.at[mine], out.at[:, :, :, columns(me)], own_sem.at[2])
    own_out.start()

    drain(near, gram_send)
    for c in range(channels - 3, channels):
        drain(arrived.at[others, pl.ds(c, 1)], in_send.at[c])
    own_out.wait()
    drain(analysed.at[others], out_send)
    drain(analysed.at[others], out_recv)


def restore(weight, z, out, staged, sem):
    per, channels, _, width = z.shape
    a, per_weight, g, _ = basis(weight)
    wide = 256
    copies = []
    for m in range(per):

        def one(b, carry):
            at = pl.ds(pl.multiple_of(b * wide, wide), wide)
            z0 = z[m, 0, :, at].astype(F32)
            rest = z[m, 1, :, at].astype(F32) * (weight[1] * per_weight)
            for c in range(2, channels):
                rest = rest + z[m, c, :, at].astype(F32) * (weight[c] * per_weight)
            staged[m, 0, :, at] = (z0 * a - rest).astype(BF16)
            shared = z0 - rest * g
            for c in range(1, channels):
                staged[m, c, :, at] = (z[m, c, :, at].astype(F32) + shared * (weight[c] * per_weight)).astype(BF16)
            return carry

        lax.fori_loop(0, width // wide, one, 0)
        copies.append(pltpu.make_async_copy(staged.at[m], out.at[m], sem.at[m]))
        copies[-1].start()
    for copy in copies:
        copy.wait()


def shards(state, obs_cell, obs_value, obs_rinv, obs_count, loc_blocks, chan_weight):
    per, channels, rows, width = state.shape
    n = lax.axis_size("mem")
    members, cols = per * n, width // n
    slots = obs_cell.shape[2]
    lanes = 128
    obs_shape = (slots // lanes, lanes)
    whole = pl.BlockSpec(memory_space=pl.ANY)
    scalars = pl.BlockSpec(memory_space=pltpu.SMEM)
    dma = pltpu.SemaphoreType.DMA
    analysed = pl.pallas_call(
        kernel,
        out_shape=pltpu.VMEM(state.shape, BF16),
        in_specs=[scalars] * 3 + [whole] * 4,
        out_specs=whole,
        scratch_shapes=[
            pltpu.VMEM(state.shape, BF16),
            pltpu.VMEM(obs_shape, jnp.int32),
            pltpu.VMEM(obs_shape, F32),
            pltpu.VMEM(obs_shape, F32),
            pltpu.VMEM((per, rows, width), F32),
            pltpu.VMEM((128, rows, cols), F32),
            pltpu.VMEM((members, 128), F32),
            pltpu.VMEM((members, 128), BF16),
            pltpu.VMEM((8, members, 128), BF16),
            pltpu.VMEM((members, channels, rows, cols), BF16),
            pltpu.VMEM((members, members * rows), BF16),
            pltpu.VMEM((members * rows, members * rows), BF16),
            pltpu.VMEM((members * rows, 2 * cols), BF16),
            pltpu.VMEM((2, rows, cols), F32),
            pltpu.VMEM((members, channels, rows, cols), BF16),
            dma((per,)),
            dma((3,)),
            dma((3,)),
            dma, dma,
            dma((channels,)),
            dma((channels,)),
            dma, dma,
        ],
        compiler_params=pltpu.CompilerParams(
            collective_id=0, has_side_effects=True, vmem_limit_bytes=63_800_000
        ),
        name="letkf",
    )(
        chan_weight, obs_count, loc_blocks[0],
        state, obs_cell.reshape(obs_shape), obs_value.reshape(obs_shape), obs_rinv.reshape(obs_shape),
    )

    return pl.pallas_call(
        restore,
        out_shape=jax.ShapeDtypeStruct(state.shape, BF16),
        in_specs=[scalars, pl.BlockSpec(memory_space=pltpu.VMEM)],
        out_specs=whole,
        scratch_shapes=[pltpu.VMEM(state.shape, BF16), dma((per,))],
        compiler_params=pltpu.CompilerParams(vmem_limit_bytes=24 * 2**20),
        name="restore",
    )(chan_weight, analysed)


def solution(mesh):
    placed = (
        P("mem", None, "lat", None),
        P("lat", "mem", None),
        P("lat", "mem", None),
        P("lat", "mem", None),
        P("lat", "mem"),
        P("lat", "mem", None),
        P(),
    )
    return jax.shard_map(
        shards, mesh=mesh, in_specs=placed, out_specs=P("mem", None, "lat", None), check_vma=False
    )
```

```python
import functools

import jax
import jax.numpy as jnp
from jax import lax
from jax.experimental import pallas as pl
from jax.experimental.pallas import tpu as pltpu
from jax.sharding import PartitionSpec as P

NS_ITERS = 5
MESH = pl.DeviceIdType.MESH
HIGHEST = lax.Precision.HIGHEST
F32 = jnp.float32
BF16 = jnp.bfloat16


def peer(me, size, index):
    step = jnp.maximum(index - 1, 0)
    distance = step // 4 + 1
    offset = jnp.where((step // 2) % 2 == 0, distance, size // 2 - distance)
    offset = jnp.where(index == 0, 0, offset)
    flip = jnp.where(index == 0, 1, step % 2)
    return ((me // 2 + offset) % (size // 2)) * 2 + (me + flip) % 2


def basis(weight):
    channels = weight.shape[0]
    big = 2.0**60
    total = (weight[0] * big) * (weight[0] * big)
    for c in range(1, channels):
        total = total + (weight[c] * big) * (weight[c] * big)
    norm = jnp.sqrt(jnp.full((8, 128), total, F32))
    some = norm > 0.0
    inverse = jnp.where(some, 1.0 / jnp.where(some, norm, 1.0), 0.0)
    first = jnp.where(some, jnp.abs(weight[0]) * big * inverse, 1.0)
    sign = jnp.where(weight[0] < 0.0, -1.0, 1.0)
    a, g = jnp.max(first), jnp.max(1.0 / (1.0 + first))
    return a, jnp.max(inverse) * big * sign, g, jnp.max(norm) * (1.0 / big) * sign


def kernel(
    weight, count, loc,
    x, cell, value, rinv,
    out,
    xv, cellv, valuev, rinvv, shared, table, gram, gram_out, near, arrived, spread, weights, perts, means, analysed,
    load_sem, obs_sem, own_sem, gram_send, gram_recv, in_send, in_recv, out_send, out_recv,
):
    n = lax.axis_size("mem")
    bands = lax.axis_size("lat")
    me, band = lax.axis_index("mem"), lax.axis_index("lat")
    per, channels, rows, width = x.shape
    members = per * n
    cols = width // n

    loads = [pltpu.make_async_copy(x.at[m], xv.at[m], load_sem.at[m]) for m in range(per)]
    for load in loads:
        load.start()
    obs_loads = [
        pltpu.make_async_copy(source, target, obs_sem.at[i])
        for i, (source, target) in enumerate(((cell, cellv), (value, valuev), (rinv, rinvv)))
    ]
    for load in obs_loads:
        load.start()

    def columns(q):
        return pl.ds(pl.multiple_of(q * cols, cols), cols)

    neighbours = [(i, j) for i in (-1, 0, 1) for j in (-1, 0, 1) if (i, j) != (0, 0)]

    def neighbour(i, j):
        return {"lat": (band + i + bands) % bands, "mem": (me + j + n) % n}

    barrier = pltpu.get_barrier_semaphore()

    def greet(i, carry):
        pl.semaphore_signal(barrier, inc=1, device_id={"mem": peer(me, n, i)}, device_id_type=MESH)
        return carry

    lax.fori_loop(0, n - 1, greet, 0)
    for i, j in neighbours:
        if i != 0:
            pl.semaphore_signal(barrier, inc=1, device_id=neighbour(i, j), device_id_type=MESH)

    a, per_weight, g, to_observed = basis(weight)
    wide = 256
    for m in range(per):
        loads[m].wait()

        def first_channel(b, carry):
            at = pl.ds(pl.multiple_of(b * wide, wide), wide)
            x0 = xv[m, 0, :, at].astype(F32)
            total = x0 * a
            for c in range(1, channels):
                total = total + xv[m, c, :, at].astype(F32) * (weight[c] * per_weight)
            xv[m, 0, :, at] = total.astype(BF16)
            shared[m, :, at] = total + x0
            return carry

        lax.fori_loop(0, width // wide, first_channel, 0)

    def other_channel(c):
        factor = weight[c] * per_weight * g

        def one(b, carry):
            at = pl.ds(pl.multiple_of(b * wide, wide), wide)
            for m in range(per):
                xv[m, c, :, at] = (xv[m, c, :, at].astype(F32) - shared[m, :, at] * factor).astype(BF16)
            return carry

        lax.fori_loop(0, width // wide, one, 0)

    pl.semaphore_wait(barrier, n - 1 + 6)

    mine = pl.ds(pl.multiple_of(me * per, per), per)

    def send_in(c):
        def one(i, carry):
            q = peer(me, n, i)
            pltpu.make_async_remote_copy(
                src_ref=xv.at[:, pl.ds(c, 1), :, columns(q)],
                dst_ref=arrived.at[mine, pl.ds(c, 1)],
                send_sem=in_send.at[c], recv_sem=in_recv.at[c],
                device_id={"mem": q}, device_id_type=MESH,
            ).start()
            return carry

        lax.fori_loop(0, n - 1, one, 0)

    def drain(ref, sem):
        pltpu.make_async_copy(ref, ref, sem).wait()

    others = pl.ds(0, members - per)

    def next_in(c):
        drain(arrived.at[others, pl.ds(c - 3, 1)], in_send.at[c - 3])
        send_in(c)

    def own_in(start, size, i):
        return pltpu.make_async_copy(
            xv.at[:, pl.ds(start, size), :, columns(me)], arrived.at[mine, pl.ds(start, size)], own_sem.at[i]
        )

    send_in(0)
    own_in(0, 1, 0).start()
    for c in (1, 2):
        other_channel(c)
        send_in(c)
    lax.fori_loop(3, channels, lambda c, carry: (other_channel(c), carry)[1], 0)
    own_in(1, channels - 1, 1).start()

    for_member = lax.broadcasted_iota(jnp.int32, (members, members * rows), 0)
    spread[...] = jnp.where(
        for_member == lax.broadcasted_iota(jnp.int32, (members, members * rows), 1) // rows, 1.0, 0.0
    ).astype(BF16)

    for load in obs_loads:
        load.wait()
    block = 8
    lanes = cellv.shape[1]
    row_of = lax.broadcasted_iota(jnp.int32, (rows, block * lanes), 0)
    col_of = lax.broadcasted_iota(jnp.int32, (cols, block * lanes), 0)

    def along(tile):
        return jnp.concatenate([tile[i : i + 1, :] for i in range(block)], axis=1)

    def histogram(b, total):
        at = pl.ds(pl.multiple_of(b * block, block), block)
        slot = (
            b * (block * lanes)
            + lax.broadcasted_iota(jnp.int32, (block, lanes), 0) * lanes
            + lax.broadcasted_iota(jnp.int32, (block, lanes), 1)
        )
        live = jnp.where(slot < count[0, 0], rinvv[at, :], 0.0)
        held = live * valuev[at, :]
        cells = along(cellv[at, :])
        hit = row_of == cells // cols
        parts = []
        for term in (live, held):
            high = term.astype(BF16).astype(F32)
            parts += [high, term - high]
        terms = jnp.concatenate([jnp.where(hit, along(part), 0.0) for part in parts], axis=0).astype(BF16)
        onehot = jnp.where(col_of == cells % cols, 1.0, 0.0).astype(BF16)
        return total + lax.dot_general(terms, onehot, (((1,), (1,)), ((), ())), preferred_element_type=F32)

    sums = lax.fori_loop(0, cellv.shape[0] // block, histogram, jnp.zeros((4 * rows, cols), F32))
    cell_rinv = sums[:rows] + sums[rows : 2 * rows]
    cell_held = sums[2 * rows : 3 * rows] + sums[3 * rows :]
    next_in(3)

    own_in(0, 1, 0).wait()
    drain(arrived.at[others, pl.ds(0, 1)], in_recv.at[0])
    step = 8
    total = jnp.zeros((rows, cols), F32)
    for k in range(0, members, step):
        total = total + jnp.sum(arrived[k : k + step, 0].astype(F32), axis=0)
    obs_mean = total * (1.0 / members)
    seen = cell_rinv > 0.0
    root_rinv = jnp.sqrt(cell_rinv)
    inverse = jnp.where(seen, 1.0 / jnp.where(seen, root_rinv, 1.0), 0.0)
    scale = root_rinv * to_observed
    for k in range(0, members, step):
        table[k : k + step] = (arrived[k : k + step, 0].astype(F32) - obs_mean[None]) * scale[None]
    tail = table.shape[0] - members
    table[members:] = jnp.zeros((tail, rows, cols), F32)
    table[members] = (cell_held - cell_rinv * (obs_mean * to_observed)) * inverse
    lines = jnp.concatenate([table[:, r, :].astype(BF16) for r in range(rows)], axis=1)
    gram[...] = lax.dot_general(lines[:members], lines, (((1,), (1,)), ((), ())), preferred_element_type=F32)
    gram_out[...] = gram[...].astype(BF16)

    for s, (i, j) in enumerate(neighbours):
        pltpu.make_async_remote_copy(
            src_ref=gram_out, dst_ref=near.at[7 - s],
            send_sem=gram_send, recv_sem=gram_recv,
            device_id=neighbour(i, j), device_id_type=MESH,
        ).start()
    next_in(4)
    next_in(5)
    drain(near, gram_recv)
    combined = gram[...] * loc[0, 4].astype(F32)
    for s, (i, j) in enumerate(neighbours):
        factor = loc[0, 3 * (i + 1) + (j + 1)]
        if i == -1:
            factor = jnp.where(band > 0, factor, 0)
        if i == 1:
            factor = jnp.where(band < bands - 1, factor, 0)
        combined = combined + factor.astype(F32) * near[s].astype(F32)

    identity = jnp.where(
        lax.broadcasted_iota(jnp.int32, (members, members), 0)
        == lax.broadcasted_iota(jnp.int32, (members, members), 1),
        1.0, 0.0,
    )

    def times(a, b):
        return jnp.dot(a, b, precision=HIGHEST, preferred_element_type=F32)

    system = (members - 1.0) * identity + combined[:, :members]
    across = combined[:, members : members + 1]
    frobenius = jnp.sqrt(jnp.sum(jnp.sum(system * system, axis=1, keepdims=True), axis=0, keepdims=True))
    current = system / frobenius

    inverse = identity
    for _ in range(NS_ITERS):
        middle = 0.5 * (3.0 * identity - times(inverse, current))
        current, inverse = times(current, middle), times(middle, inverse)
    root = inverse / jnp.sqrt(frobenius)
    half = jnp.sum(root * across, axis=0, keepdims=True)
    half = jnp.sum(identity * half, axis=1, keepdims=True)
    shift = jnp.sum(root * half, axis=0, keepdims=True)
    transform = (float(members - 1) ** 0.5 * root + shift).astype(BF16)
    next_in(6)

    tall = 128
    repeated = jnp.dot(transform, spread[...], preferred_element_type=F32).astype(BF16)

    def expand(b, carry):
        at = lax.broadcasted_iota(jnp.int32, (tall, members), 0) + b * tall
        pick = jnp.where(
            at // rows == lax.broadcasted_iota(jnp.int32, (tall, members), 1), 1.0, 0.0
        ).astype(BF16)
        full = jnp.dot(pick, repeated, preferred_element_type=F32)
        same = (
            lax.broadcasted_iota(jnp.int32, full.shape, 0) % rows
            == lax.broadcasted_iota(jnp.int32, full.shape, 1) % rows
        )
        weights[pl.ds(pl.multiple_of(b * tall, tall), tall), :] = jnp.where(same, full, 0.0).astype(BF16)
        return carry

    lax.fori_loop(0, members * rows // tall, expand, 0)
    lax.fori_loop(7, channels, lambda c, carry: (next_in(c), carry)[1], 0)
    own_in(1, channels - 1, 1).wait()

    high = 256

    def analyse(p, carry):
        for h in range(2):
            c = 2 * p + h
            if h == 0:
                @pl.when(p > 0)
                def _():
                    drain(arrived.at[others, pl.ds(c, 1)], in_recv.at[c])
            else:
                drain(arrived.at[others, pl.ds(c, 1)], in_recv.at[c])
            total = jnp.zeros((rows, cols), F32)
            for k in range(0, members, step):
                total = total + jnp.sum(arrived[k : k + step, c].astype(F32), axis=0)
            mean = total * (1.0 / members)
            means[h] = mean
            for k in range(0, members, step):
                part = (arrived[k : k + step, c].astype(F32) - mean[None]).astype(BF16)
                perts[k * rows : (k + step) * rows, h * cols : (h + 1) * cols] = part.reshape(step * rows, cols)

        def mix(b, inner):
            at = pl.ds(pl.multiple_of(b * high, high), high)
            shifted = jnp.dot(weights[at, :], perts[...], preferred_element_type=F32)
            for h in range(2):
                part = shifted[:, h * cols : (h + 1) * cols].reshape(high // rows, rows, cols) + means[h][None]
                analysed[pl.ds(b * (high // rows), high // rows), 2 * p + h] = part.astype(BF16)
            return inner

        lax.fori_loop(0, members * rows // high, mix, 0)

        def one(i, inner):
            last = (p == channels // 2 - 1).astype(jnp.int32)
            fixed = jnp.where(i < 5, i + 1, jnp.where(i == 5, 0, i))
            q = jnp.where(last == 1, fixed, peer(me, n, jnp.minimum(i, n - 2)))

            @pl.when(jnp.where(last == 1, (q != me).astype(jnp.int32), (i < n - 1).astype(jnp.int32)) == 1)
            def _():
                pltpu.make_async_remote_copy(
                    src_ref=analysed.at[pl.ds(q * per, per), pl.ds(2 * p, 2)],
                    dst_ref=out.at[:, pl.ds(2 * p, 2), :, columns(me)],
                    send_sem=out_send, recv_sem=out_recv,
                    device_id={"mem": q}, device_id_type=MESH,
                ).start()

            return inner

        lax.fori_loop(0, n, one, 0)
        return carry

    lax.fori_loop(0, channels // 2, analyse, 0)
    own_out = pltpu.make_async_copy(analysed.at[mine], out.at[:, :, :, columns(me)], own_sem.at[2])
    own_out.start()

    drain(near, gram_send)
    for c in range(channels - 3, channels):
        drain(arrived.at[others, pl.ds(c, 1)], in_send.at[c])
    own_out.wait()
    drain(analysed.at[others], out_send)
    drain(analysed.at[others], out_recv)


def restore(weight, z, out, staged, sem):
    per, channels, _, width = z.shape
    a, per_weight, g, _ = basis(weight)
    wide = 256
    copies = []
    for m in range(per):

        def one(b, carry):
            at = pl.ds(pl.multiple_of(b * wide, wide), wide)
            z0 = z[m, 0, :, at].astype(F32)
            rest = z[m, 1, :, at].astype(F32) * (weight[1] * per_weight)
            for c in range(2, channels):
                rest = rest + z[m, c, :, at].astype(F32) * (weight[c] * per_weight)
            staged[m, 0, :, at] = (z0 * a - rest).astype(BF16)
            shared = z0 - rest * g
            for c in range(1, channels):
                staged[m, c, :, at] = (z[m, c, :, at].astype(F32) + shared * (weight[c] * per_weight)).astype(BF16)
            return carry

        lax.fori_loop(0, width // wide, one, 0)
        copies.append(pltpu.make_async_copy(staged.at[m], out.at[m], sem.at[m]))
        copies[-1].start()
    for copy in copies:
        copy.wait()


def shards(state, obs_cell, obs_value, obs_rinv, obs_count, loc_blocks, chan_weight):
    per, channels, rows, width = state.shape
    n = lax.axis_size("mem")
    members, cols = per * n, width // n
    slots = obs_cell.shape[2]
    lanes = 128
    obs_shape = (slots // lanes, lanes)
    whole = pl.BlockSpec(memory_space=pl.ANY)
    scalars = pl.BlockSpec(memory_space=pltpu.SMEM)
    dma = pltpu.SemaphoreType.DMA
    analysed = pl.pallas_call(
        kernel,
        out_shape=pltpu.VMEM(state.shape, BF16),
        in_specs=[scalars] * 3 + [whole] * 4,
        out_specs=whole,
        scratch_shapes=[
            pltpu.VMEM(state.shape, BF16),
            pltpu.VMEM(obs_shape, jnp.int32),
            pltpu.VMEM(obs_shape, F32),
            pltpu.VMEM(obs_shape, F32),
            pltpu.VMEM((per, rows, width), F32),
            pltpu.VMEM((128, rows, cols), F32),
            pltpu.VMEM((members, 128), F32),
            pltpu.VMEM((members, 128), BF16),
            pltpu.VMEM((8, members, 128), BF16),
            pltpu.VMEM((members, channels, rows, cols), BF16),
            pltpu.VMEM((members, members * rows), BF16),
            pltpu.VMEM((members * rows, members * rows), BF16),
            pltpu.VMEM((members * rows, 2 * cols), BF16),
            pltpu.VMEM((2, rows, cols), F32),
            pltpu.VMEM((members, channels, rows, cols), BF16),
            dma((per,)),
            dma((3,)),
            dma((3,)),
            dma, dma,
            dma((channels,)),
            dma((channels,)),
            dma, dma,
        ],
        compiler_params=pltpu.CompilerParams(
            collective_id=0, has_side_effects=True, vmem_limit_bytes=63_800_000
        ),
        name="letkf",
    )(
        chan_weight, obs_count, loc_blocks[0],
        state, obs_cell.reshape(obs_shape), obs_value.reshape(obs_shape), obs_rinv.reshape(obs_shape),
    )

    return pl.pallas_call(
        restore,
        out_shape=jax.ShapeDtypeStruct(state.shape, BF16),
        in_specs=[scalars, pl.BlockSpec(memory_space=pltpu.VMEM)],
        out_specs=whole,
        scratch_shapes=[pltpu.VMEM(state.shape, BF16), dma((per,))],
        compiler_params=pltpu.CompilerParams(vmem_limit_bytes=24 * 2**20),
        name="restore",
    )(chan_weight, analysed)


def solution(mesh):
    placed = (
        P("mem", None, "lat", None),
        P("lat", "mem", None),
        P("lat", "mem", None),
        P("lat", "mem", None),
        P("lat", "mem"),
        P("lat", "mem", None),
        P(),
    )
    return jax.shard_map(
        shards, mesh=mesh, in_specs=placed, out_specs=P("mem", None, "lat", None), check_vma=False
    )
```

```python
import functools

import jax
import jax.numpy as jnp
from jax import lax
from jax.experimental import pallas as pl
from jax.experimental.pallas import tpu as pltpu
from jax.sharding import PartitionSpec as P

NS_ITERS = 5
MESH = pl.DeviceIdType.MESH
HIGHEST = lax.Precision.HIGHEST
F32 = jnp.float32
BF16 = jnp.bfloat16


def peer(me, size, index):
    step = jnp.maximum(index - 1, 0)
    distance = step // 4 + 1
    offset = jnp.where((step // 2) % 2 == 0, distance, size // 2 - distance)
    offset = jnp.where(index == 0, 0, offset)
    flip = jnp.where(index == 0, 1, step % 2)
    return ((me // 2 + offset) % (size // 2)) * 2 + (me + flip) % 2


def basis(weight):
    channels = weight.shape[0]
    big = 2.0**60
    total = (weight[0] * big) * (weight[0] * big)
    for c in range(1, channels):
        total = total + (weight[c] * big) * (weight[c] * big)
    norm = jnp.sqrt(jnp.full((8, 128), total, F32))
    some = norm > 0.0
    inverse = jnp.where(some, 1.0 / jnp.where(some, norm, 1.0), 0.0)
    first = jnp.where(some, jnp.abs(weight[0]) * big * inverse, 1.0)
    sign = jnp.where(weight[0] < 0.0, -1.0, 1.0)
    a, g = jnp.max(first), jnp.max(1.0 / (1.0 + first))
    return a, jnp.max(inverse) * big * sign, g, jnp.max(norm) * (1.0 / big) * sign


def kernel(
    weight_in, count_in, loc_in, x, cell, value, rinv,
    out,
    weight, count, loc, xv, cellv, valuev, rinvv, shared, table, gram, gram_out, near, arrived, spread, weights, perts, means, analysed,
    scalar_sem, load_sem, obs_sem, own_sem, gram_send, gram_recv, in_send, in_recv, out_send, out_recv,
):
    n = lax.axis_size("mem")
    bands = lax.axis_size("lat")
    me, band = lax.axis_index("mem"), lax.axis_index("lat")
    per, channels, rows, width = x.shape
    members = per * n
    cols = width // n

    def columns(q):
        return pl.ds(pl.multiple_of(q * cols, cols), cols)

    neighbours = [(i, j) for i in (-1, 0, 1) for j in (-1, 0, 1) if (i, j) != (0, 0)]

    def neighbour(i, j):
        return {"lat": (band + i + bands) % bands, "mem": (me + j + n) % n}

    barrier = pltpu.get_barrier_semaphore()

    def greet(i, carry):
        pl.semaphore_signal(barrier, inc=1, device_id={"mem": peer(me, n, i)}, device_id_type=MESH)
        return carry

    lax.fori_loop(0, n - 1, greet, 0)
    for i, j in neighbours:
        if i != 0:
            pl.semaphore_signal(barrier, inc=1, device_id=neighbour(i, j), device_id_type=MESH)

    scalar_loads = [
        pltpu.make_async_copy(source, target, scalar_sem.at[i])
        for i, (source, target) in enumerate(((weight_in, weight), (count_in, count), (loc_in, loc)))
    ]
    for load in scalar_loads:
        load.start()
    loads = [pltpu.make_async_copy(x.at[m], xv.at[m], load_sem.at[m]) for m in range(per)]
    for load in loads:
        load.start()
    obs_loads = [
        pltpu.make_async_copy(source, target, obs_sem.at[i])
        for i, (source, target) in enumerate(((cell, cellv), (value, valuev), (rinv, rinvv)))
    ]
    for load in obs_loads:
        load.start()

    for load in scalar_loads:
        load.wait()

    a, per_weight, g, to_observed = basis(weight)
    wide = 256
    for m in range(per):
        loads[m].wait()

        def first_channel(b, carry):
            at = pl.ds(pl.multiple_of(b * wide, wide), wide)
            x0 = xv[m, 0, :, at].astype(F32)
            total = x0 * a
            for c in range(1, channels):
                total = total + xv[m, c, :, at].astype(F32) * (weight[c] * per_weight)
            xv[m, 0, :, at] = total.astype(BF16)
            shared[m, :, at] = total + x0
            return carry

        lax.fori_loop(0, width // wide, first_channel, 0)

    def other_channel(c):
        factor = weight[c] * per_weight * g

        def one(b, carry):
            at = pl.ds(pl.multiple_of(b * wide, wide), wide)
            for m in range(per):
                xv[m, c, :, at] = (xv[m, c, :, at].astype(F32) - shared[m, :, at] * factor).astype(BF16)
            return carry

        lax.fori_loop(0, width // wide, one, 0)

    pl.semaphore_wait(barrier, n - 1 + 6)

    mine = pl.ds(pl.multiple_of(me * per, per), per)

    def send_in(c):
        def one(i, carry):
            q = peer(me, n, i)
            pltpu.make_async_remote_copy(
                src_ref=xv.at[:, pl.ds(c, 1), :, columns(q)],
                dst_ref=arrived.at[mine, pl.ds(c, 1)],
                send_sem=in_send.at[c], recv_sem=in_recv.at[c],
                device_id={"mem": q}, device_id_type=MESH,
            ).start()
            return carry

        lax.fori_loop(0, n - 1, one, 0)

    def drain(ref, sem):
        pltpu.make_async_copy(ref, ref, sem).wait()

    others = pl.ds(0, members - per)

    def next_in(c):
        drain(arrived.at[others, pl.ds(c - 3, 1)], in_send.at[c - 3])
        send_in(c)

    def own_in(start, size, i):
        return pltpu.make_async_copy(
            xv.at[:, pl.ds(start, size), :, columns(me)], arrived.at[mine, pl.ds(start, size)], own_sem.at[i]
        )

    send_in(0)
    own_in(0, 1, 0).start()
    for c in (1, 2):
        other_channel(c)
        send_in(c)
    lax.fori_loop(3, channels, lambda c, carry: (other_channel(c), carry)[1], 0)
    own_in(1, channels - 1, 1).start()

    for_member = lax.broadcasted_iota(jnp.int32, (members, members * rows), 0)
    spread[...] = jnp.where(
        for_member == lax.broadcasted_iota(jnp.int32, (members, members * rows), 1) // rows, 1.0, 0.0
    ).astype(BF16)

    for load in obs_loads:
        load.wait()
    block = 8
    lanes = cellv.shape[1]
    row_of = lax.broadcasted_iota(jnp.int32, (rows, block * lanes), 0)
    col_of = lax.broadcasted_iota(jnp.int32, (cols, block * lanes), 0)

    def along(tile):
        return jnp.concatenate([tile[i : i + 1, :] for i in range(block)], axis=1)

    def histogram(b, total):
        at = pl.ds(pl.multiple_of(b * block, block), block)
        slot = (
            b * (block * lanes)
            + lax.broadcasted_iota(jnp.int32, (block, lanes), 0) * lanes
            + lax.broadcasted_iota(jnp.int32, (block, lanes), 1)
        )
        live = jnp.where(slot < count[0, 0], rinvv[at, :], 0.0)
        held = live * valuev[at, :]
        cells = along(cellv[at, :])
        hit = row_of == cells // cols
        parts = []
        for term in (live, held):
            high = term.astype(BF16).astype(F32)
            parts += [high, term - high]
        terms = jnp.concatenate([jnp.where(hit, along(part), 0.0) for part in parts], axis=0).astype(BF16)
        onehot = jnp.where(col_of == cells % cols, 1.0, 0.0).astype(BF16)
        return total + lax.dot_general(terms, onehot, (((1,), (1,)), ((), ())), preferred_element_type=F32)

    sums = lax.fori_loop(0, cellv.shape[0] // block, histogram, jnp.zeros((4 * rows, cols), F32))
    cell_rinv = sums[:rows] + sums[rows : 2 * rows]
    cell_held = sums[2 * rows : 3 * rows] + sums[3 * rows :]
    next_in(3)

    own_in(0, 1, 0).wait()
    drain(arrived.at[others, pl.ds(0, 1)], in_recv.at[0])
    step = 8
    total = jnp.zeros((rows, cols), F32)
    for k in range(0, members, step):
        total = total + jnp.sum(arrived[k : k + step, 0].astype(F32), axis=0)
    obs_mean = total * (1.0 / members)
    seen = cell_rinv > 0.0
    root_rinv = jnp.sqrt(cell_rinv)
    inverse = jnp.where(seen, 1.0 / jnp.where(seen, root_rinv, 1.0), 0.0)
    scale = root_rinv * to_observed
    for k in range(0, members, step):
        table[k : k + step] = (arrived[k : k + step, 0].astype(F32) - obs_mean[None]) * scale[None]
    tail = table.shape[0] - members
    table[members:] = jnp.zeros((tail, rows, cols), F32)
    table[members] = (cell_held - cell_rinv * (obs_mean * to_observed)) * inverse
    lines = jnp.concatenate([table[:, r, :].astype(BF16) for r in range(rows)], axis=1)
    gram[...] = lax.dot_general(lines[:members], lines, (((1,), (1,)), ((), ())), preferred_element_type=F32)
    gram_out[...] = gram[...].astype(BF16)

    for s, (i, j) in enumerate(neighbours):
        pltpu.make_async_remote_copy(
            src_ref=gram_out, dst_ref=near.at[7 - s],
            send_sem=gram_send, recv_sem=gram_recv,
            device_id=neighbour(i, j), device_id_type=MESH,
        ).start()
    next_in(4)
    next_in(5)
    drain(near, gram_recv)
    combined = gram[...] * loc[0, 4].astype(F32)
    for s, (i, j) in enumerate(neighbours):
        factor = loc[0, 3 * (i + 1) + (j + 1)]
        if i == -1:
            factor = jnp.where(band > 0, factor, 0)
        if i == 1:
            factor = jnp.where(band < bands - 1, factor, 0)
        combined = combined + factor.astype(F32) * near[s].astype(F32)

    identity = jnp.where(
        lax.broadcasted_iota(jnp.int32, (members, members), 0)
        == lax.broadcasted_iota(jnp.int32, (members, members), 1),
        1.0, 0.0,
    )

    def times(a, b):
        return jnp.dot(a, b, precision=HIGHEST, preferred_element_type=F32)

    system = (members - 1.0) * identity + combined[:, :members]
    across = combined[:, members : members + 1]
    frobenius = jnp.sqrt(jnp.sum(jnp.sum(system * system, axis=1, keepdims=True), axis=0, keepdims=True))
    current = system / frobenius

    inverse = identity
    for _ in range(NS_ITERS):
        middle = 0.5 * (3.0 * identity - times(inverse, current))
        current, inverse = times(current, middle), times(middle, inverse)
    root = inverse / jnp.sqrt(frobenius)
    half = jnp.sum(root * across, axis=0, keepdims=True)
    half = jnp.sum(identity * half, axis=1, keepdims=True)
    shift = jnp.sum(root * half, axis=0, keepdims=True)
    transform = (float(members - 1) ** 0.5 * root + shift).astype(BF16)
    next_in(6)

    tall = 128
    repeated = jnp.dot(transform, spread[...], preferred_element_type=F32).astype(BF16)

    def expand(b, carry):
        at = lax.broadcasted_iota(jnp.int32, (tall, members), 0) + b * tall
        pick = jnp.where(
            at // rows == lax.broadcasted_iota(jnp.int32, (tall, members), 1), 1.0, 0.0
        ).astype(BF16)
        full = jnp.dot(pick, repeated, preferred_element_type=F32)
        same = (
            lax.broadcasted_iota(jnp.int32, full.shape, 0) % rows
            == lax.broadcasted_iota(jnp.int32, full.shape, 1) % rows
        )
        weights[pl.ds(pl.multiple_of(b * tall, tall), tall), :] = jnp.where(same, full, 0.0).astype(BF16)
        return carry

    lax.fori_loop(0, members * rows // tall, expand, 0)
    lax.fori_loop(7, channels, lambda c, carry: (next_in(c), carry)[1], 0)
    own_in(1, channels - 1, 1).wait()

    high = 256

    def analyse(p, carry):
        for h in range(2):
            c = 2 * p + h
            if h == 0:
                @pl.when(p > 0)
                def _():
                    drain(arrived.at[others, pl.ds(c, 1)], in_recv.at[c])
            else:
                drain(arrived.at[others, pl.ds(c, 1)], in_recv.at[c])
            total = jnp.zeros((rows, cols), F32)
            for k in range(0, members, step):
                total = total + jnp.sum(arrived[k : k + step, c].astype(F32), axis=0)
            mean = total * (1.0 / members)
            means[h] = mean
            for k in range(0, members, step):
                part = (arrived[k : k + step, c].astype(F32) - mean[None]).astype(BF16)
                perts[k * rows : (k + step) * rows, h * cols : (h + 1) * cols] = part.reshape(step * rows, cols)

        def mix(b, inner):
            at = pl.ds(pl.multiple_of(b * high, high), high)
            shifted = jnp.dot(weights[at, :], perts[...], preferred_element_type=F32)
            for h in range(2):
                part = shifted[:, h * cols : (h + 1) * cols].reshape(high // rows, rows, cols) + means[h][None]
                analysed[pl.ds(b * (high // rows), high // rows), 2 * p + h] = part.astype(BF16)
            return inner

        lax.fori_loop(0, members * rows // high, mix, 0)

        def one(i, inner):
            last = (p == channels // 2 - 1).astype(jnp.int32)
            fixed = jnp.where(i < 5, i + 1, jnp.where(i == 5, 0, i))
            q = jnp.where(last == 1, fixed, peer(me, n, jnp.minimum(i, n - 2)))

            @pl.when(jnp.where(last == 1, (q != me).astype(jnp.int32), (i < n - 1).astype(jnp.int32)) == 1)
            def _():
                pltpu.make_async_remote_copy(
                    src_ref=analysed.at[pl.ds(q * per, per), pl.ds(2 * p, 2)],
                    dst_ref=out.at[:, pl.ds(2 * p, 2), :, columns(me)],
                    send_sem=out_send, recv_sem=out_recv.at[jnp.where(last == 1, me, n)],
                    device_id={"mem": q}, device_id_type=MESH,
                ).start()

            return inner

        lax.fori_loop(0, n, one, 0)
        return carry

    lax.fori_loop(0, channels // 2, analyse, 0)
    own_out = pltpu.make_async_copy(analysed.at[mine], out.at[:, :, :, columns(me)], own_sem.at[2])
    own_out.start()

    drain(near, gram_send)
    for c in range(channels - 3, channels):
        drain(arrived.at[others, pl.ds(c, 1)], in_send.at[c])
    drain(analysed.at[others, pl.ds(0, channels - 2)], out_recv.at[n])
    own_out.wait()

    def term(m, c, q):
        return out[m, c, :, columns(q)].astype(F32) * (weight[c] * per_weight)

    def gather(q, carry):
        for m in range(per):
            rest = term(m, 1, q)
            for c in range(2, channels - 2):
                rest = rest + term(m, c, q)
            shared[m, :, columns(q)] = rest
        return carry

    lax.fori_loop(0, n, gather, 0)

    def restore(q):
        for m in range(per):
            z0 = out[m, 0, :, columns(q)].astype(F32)
            rest = shared[m, :, columns(q)] + (term(m, channels - 2, q) + term(m, channels - 1, q))
            out[m, 0, :, columns(q)] = (z0 * a - rest).astype(BF16)
            common = z0 - rest * g
            for c in range(1, channels):
                kept = out[m, c, :, columns(q)].astype(F32)
                out[m, c, :, columns(q)] = (kept + common * (weight[c] * per_weight)).astype(BF16)

    restore(me)

    def take(i, carry):
        q = peer(me, n, i)
        drain(out.at[:, pl.ds(channels - 2, 2), :, columns(q)], out_recv.at[q])
        restore(q)
        return carry

    lax.fori_loop(0, n - 1, take, 0)
    drain(analysed.at[others], out_send)


def put(z, out, sem):
    per, channels, _, _ = z.shape
    half = channels // 2
    copies = [
        pltpu.make_async_copy(
            z.at[m, pl.ds(h * half, half)], out.at[m, pl.ds(h * half, half)], sem.at[2 * m + h]
        )
        for m in range(per)
        for h in range(2)
    ]
    for copy in copies:
        copy.start()
    for copy in copies:
        copy.wait()


def shards(state, obs_cell, obs_value, obs_rinv, obs_count, loc_blocks, chan_weight):
    per, channels, rows, width = state.shape
    n = lax.axis_size("mem")
    members, cols = per * n, width // n
    slots = obs_cell.shape[2]
    lanes = 128
    obs_shape = (slots // lanes, lanes)
    whole = pl.BlockSpec(memory_space=pl.ANY)
    dma = pltpu.SemaphoreType.DMA
    analysed = pl.pallas_call(
        kernel,
        out_shape=pltpu.VMEM(state.shape, BF16),
        in_specs=[whole] * 7,
        out_specs=pl.BlockSpec(memory_space=pltpu.VMEM),
        scratch_shapes=[
            pltpu.SMEM(chan_weight.shape, F32),
            pltpu.SMEM((1, 1), jnp.int32),
            pltpu.SMEM((1, 9), jnp.int32),
            pltpu.VMEM(state.shape, BF16),
            pltpu.VMEM(obs_shape, jnp.int32),
            pltpu.VMEM(obs_shape, F32),
            pltpu.VMEM(obs_shape, F32),
            pltpu.VMEM((per, rows, width), F32),
            pltpu.VMEM((128, rows, cols), F32),
            pltpu.VMEM((members, 128), F32),
            pltpu.VMEM((members, 128), BF16),
            pltpu.VMEM((8, members, 128), BF16),
            pltpu.VMEM((members, channels, rows, cols), BF16),
            pltpu.VMEM((members, members * rows), BF16),
            pltpu.VMEM((members * rows, members * rows), BF16),
            pltpu.VMEM((members * rows, 2 * cols), BF16),
            pltpu.VMEM((2, rows, cols), F32),
            pltpu.VMEM((members, channels, rows, cols), BF16),
            dma((3,)),
            dma((per,)),
            dma((3,)),
            dma((3,)),
            dma, dma,
            dma((channels,)),
            dma((channels,)),
            dma,
            dma((n + 1,)),
        ],
        compiler_params=pltpu.CompilerParams(
            collective_id=0, has_side_effects=True, vmem_limit_bytes=63_800_000
        ),
        name="letkf",
    )(
        chan_weight, obs_count, loc_blocks[0],
        state, obs_cell.reshape(obs_shape), obs_value.reshape(obs_shape), obs_rinv.reshape(obs_shape),
    )

    return pl.pallas_call(
        put,
        out_shape=jax.ShapeDtypeStruct(state.shape, BF16),
        in_specs=[pl.BlockSpec(memory_space=pltpu.VMEM)],
        out_specs=whole,
        scratch_shapes=[dma((2 * per,))],
        compiler_params=pltpu.CompilerParams(vmem_limit_bytes=24 * 2**20),
        name="put",
    )(analysed)


def solution(mesh):
    placed = (
        P("mem", None, "lat", None),
        P("lat", "mem", None),
        P("lat", "mem", None),
        P("lat", "mem", None),
        P("lat", "mem"),
        P("lat", "mem", None),
        P(),
    )
    return jax.shard_map(
        shards, mesh=mesh, in_specs=placed, out_specs=P("mem", None, "lat", None), check_vma=False
    )
```

```python
import functools

import jax
import jax.numpy as jnp
from jax import lax
from jax.experimental import pallas as pl
from jax.experimental.pallas import tpu as pltpu
from jax.sharding import PartitionSpec as P

NS_ITERS = 5
MESH = pl.DeviceIdType.MESH
HIGHEST = lax.Precision.HIGHEST
F32 = jnp.float32
BF16 = jnp.bfloat16


def peer(me, size, index):
    step = jnp.maximum(index - 1, 0)
    distance = step // 4 + 1
    offset = jnp.where((step // 2) % 2 == 0, distance, size // 2 - distance)
    offset = jnp.where(index == 0, 0, offset)
    flip = jnp.where(index == 0, 1, step % 2)
    return ((me // 2 + offset) % (size // 2)) * 2 + (me + flip) % 2


def basis(weight):
    channels = weight.shape[0]
    big = 2.0**60
    total = (weight[0] * big) * (weight[0] * big)
    for c in range(1, channels):
        total = total + (weight[c] * big) * (weight[c] * big)
    norm = jnp.sqrt(jnp.full((8, 128), total, F32))
    some = norm > 0.0
    inverse = jnp.where(some, 1.0 / jnp.where(some, norm, 1.0), 0.0)
    first = jnp.where(some, jnp.abs(weight[0]) * big * inverse, 1.0)
    sign = jnp.where(weight[0] < 0.0, -1.0, 1.0)
    a, g = jnp.max(first), jnp.max(1.0 / (1.0 + first))
    return a, jnp.max(inverse) * big * sign, g, jnp.max(norm) * (1.0 / big) * sign


def kernel(
    weight_in, count_in, loc_in, x, cell, value, rinv,
    out,
    weight, count, loc, xv, cellv, valuev, rinvv, shared, table, gram, gram_out, near, arrived, spread, weights, perts, means, analysed,
    scalar_sem, load_sem, obs_sem, own_sem, gram_send, gram_recv, in_send, in_recv, out_send, out_recv,
):
    n = lax.axis_size("mem")
    bands = lax.axis_size("lat")
    me, band = lax.axis_index("mem"), lax.axis_index("lat")
    per, channels, rows, width = x.shape
    members = per * n
    cols = width // n

    def columns(q):
        return pl.ds(pl.multiple_of(q * cols, cols), cols)

    neighbours = [(i, j) for i in (-1, 0, 1) for j in (-1, 0, 1) if (i, j) != (0, 0)]

    def neighbour(i, j):
        return {"lat": (band + i + bands) % bands, "mem": (me + j + n) % n}

    barrier = pltpu.get_barrier_semaphore()

    def greet(i, carry):
        pl.semaphore_signal(barrier, inc=1, device_id={"mem": peer(me, n, i)}, device_id_type=MESH)
        return carry

    lax.fori_loop(0, n - 1, greet, 0)
    for i, j in neighbours:
        if i != 0:
            pl.semaphore_signal(barrier, inc=1, device_id=neighbour(i, j), device_id_type=MESH)

    scalar_loads = [
        pltpu.make_async_copy(source, target, scalar_sem.at[i])
        for i, (source, target) in enumerate(((weight_in, weight), (count_in, count), (loc_in, loc)))
    ]
    for load in scalar_loads:
        load.start()
    loads = [pltpu.make_async_copy(x.at[m], xv.at[m], load_sem.at[m]) for m in range(per)]
    for load in loads:
        load.start()
    obs_loads = [
        pltpu.make_async_copy(source, target, obs_sem.at[i])
        for i, (source, target) in enumerate(((cell, cellv), (value, valuev), (rinv, rinvv)))
    ]
    for load in obs_loads:
        load.start()

    for load in scalar_loads:
        load.wait()

    a, per_weight, g, to_observed = basis(weight)
    wide = 256
    for m in range(per):
        loads[m].wait()

        def first_channel(b, carry):
            at = pl.ds(pl.multiple_of(b * wide, wide), wide)
            x0 = xv[m, 0, :, at].astype(F32)
            total = x0 * a
            for c in range(1, channels):
                total = total + xv[m, c, :, at].astype(F32) * (weight[c] * per_weight)
            xv[m, 0, :, at] = total.astype(BF16)
            shared[m, :, at] = total + x0
            return carry

        lax.fori_loop(0, width // wide, first_channel, 0)

    def other_channel(c):
        factor = weight[c] * per_weight * g

        def one(b, carry):
            at = pl.ds(pl.multiple_of(b * wide, wide), wide)
            for m in range(per):
                xv[m, c, :, at] = (xv[m, c, :, at].astype(F32) - shared[m, :, at] * factor).astype(BF16)
            return carry

        lax.fori_loop(0, width // wide, one, 0)

    pl.semaphore_wait(barrier, n - 1 + 6)

    mine = pl.ds(pl.multiple_of(me * per, per), per)

    def send_in(c):
        def one(i, carry):
            q = peer(me, n, i)
            pltpu.make_async_remote_copy(
                src_ref=xv.at[:, pl.ds(c, 1), :, columns(q)],
                dst_ref=arrived.at[mine, pl.ds(c, 1)],
                send_sem=in_send.at[c], recv_sem=in_recv.at[c],
                device_id={"mem": q}, device_id_type=MESH,
            ).start()
            return carry

        lax.fori_loop(0, n - 1, one, 0)

    def drain(ref, sem):
        pltpu.make_async_copy(ref, ref, sem).wait()

    others = pl.ds(0, members - per)

    def next_in(c):
        drain(arrived.at[others, pl.ds(c - 3, 1)], in_send.at[c - 3])
        send_in(c)

    def own_in(start, size, i):
        return pltpu.make_async_copy(
            xv.at[:, pl.ds(start, size), :, columns(me)], arrived.at[mine, pl.ds(start, size)], own_sem.at[i]
        )

    send_in(0)
    own_in(0, 1, 0).start()
    for c in (1, 2):
        other_channel(c)
        send_in(c)
    lax.fori_loop(3, channels, lambda c, carry: (other_channel(c), carry)[1], 0)
    own_in(1, channels - 1, 1).start()

    for_member = lax.broadcasted_iota(jnp.int32, (members, members * rows), 0)
    spread[...] = jnp.where(
        for_member == lax.broadcasted_iota(jnp.int32, (members, members * rows), 1) // rows, 1.0, 0.0
    ).astype(BF16)

    for load in obs_loads:
        load.wait()
    block = 8
    lanes = cellv.shape[1]
    row_of = lax.broadcasted_iota(jnp.int32, (rows, block * lanes), 0)
    col_of = lax.broadcasted_iota(jnp.int32, (cols, block * lanes), 0)

    def along(tile):
        return jnp.concatenate([tile[i : i + 1, :] for i in range(block)], axis=1)

    def histogram(b, total):
        at = pl.ds(pl.multiple_of(b * block, block), block)
        slot = (
            b * (block * lanes)
            + lax.broadcasted_iota(jnp.int32, (block, lanes), 0) * lanes
            + lax.broadcasted_iota(jnp.int32, (block, lanes), 1)
        )
        live = jnp.where(slot < count[0, 0], rinvv[at, :], 0.0)
        held = live * valuev[at, :]
        cells = along(cellv[at, :])
        hit = row_of == cells // cols
        parts = []
        for term in (live, held):
            high = term.astype(BF16).astype(F32)
            parts += [high, term - high]
        terms = jnp.concatenate([jnp.where(hit, along(part), 0.0) for part in parts], axis=0).astype(BF16)
        onehot = jnp.where(col_of == cells % cols, 1.0, 0.0).astype(BF16)
        return total + lax.dot_general(terms, onehot, (((1,), (1,)), ((), ())), preferred_element_type=F32)

    sums = lax.fori_loop(0, cellv.shape[0] // block, histogram, jnp.zeros((4 * rows, cols), F32))
    cell_rinv = sums[:rows] + sums[rows : 2 * rows]
    cell_held = sums[2 * rows : 3 * rows] + sums[3 * rows :]
    next_in(3)

    own_in(0, 1, 0).wait()
    drain(arrived.at[others, pl.ds(0, 1)], in_recv.at[0])
    step = 8
    total = jnp.zeros((rows, cols), F32)
    for k in range(0, members, step):
        total = total + jnp.sum(arrived[k : k + step, 0].astype(F32), axis=0)
    obs_mean = total * (1.0 / members)
    seen = cell_rinv > 0.0
    root_rinv = jnp.sqrt(cell_rinv)
    inverse = jnp.where(seen, 1.0 / jnp.where(seen, root_rinv, 1.0), 0.0)
    scale = root_rinv * to_observed
    for k in range(0, members, step):
        table[k : k + step] = (arrived[k : k + step, 0].astype(F32) - obs_mean[None]) * scale[None]
    tail = table.shape[0] - members
    table[members:] = jnp.zeros((tail, rows, cols), F32)
    table[members] = (cell_held - cell_rinv * (obs_mean * to_observed)) * inverse
    lines = jnp.concatenate([table[:, r, :].astype(BF16) for r in range(rows)], axis=1)
    gram[...] = lax.dot_general(lines[:members], lines, (((1,), (1,)), ((), ())), preferred_element_type=F32)
    gram_out[...] = gram[...].astype(BF16)

    for s, (i, j) in enumerate(neighbours):
        pltpu.make_async_remote_copy(
            src_ref=gram_out, dst_ref=near.at[7 - s],
            send_sem=gram_send, recv_sem=gram_recv,
            device_id=neighbour(i, j), device_id_type=MESH,
        ).start()
    next_in(4)
    next_in(5)
    drain(near, gram_recv)
    combined = gram[...] * loc[0, 4].astype(F32)
    for s, (i, j) in enumerate(neighbours):
        factor = loc[0, 3 * (i + 1) + (j + 1)]
        if i == -1:
            factor = jnp.where(band > 0, factor, 0)
        if i == 1:
            factor = jnp.where(band < bands - 1, factor, 0)
        combined = combined + factor.astype(F32) * near[s].astype(F32)

    identity = jnp.where(
        lax.broadcasted_iota(jnp.int32, (members, members), 0)
        == lax.broadcasted_iota(jnp.int32, (members, members), 1),
        1.0, 0.0,
    )

    def times(a, b):
        return jnp.dot(a, b, precision=HIGHEST, preferred_element_type=F32)

    system = (members - 1.0) * identity + combined[:, :members]
    across = combined[:, members : members + 1]
    frobenius = jnp.sqrt(jnp.sum(jnp.sum(system * system, axis=1, keepdims=True), axis=0, keepdims=True))
    current = system / frobenius

    inverse = identity
    for _ in range(NS_ITERS):
        middle = 0.5 * (3.0 * identity - times(inverse, current))
        current, inverse = times(current, middle), times(middle, inverse)
    root = inverse / jnp.sqrt(frobenius)
    half = jnp.sum(root * across, axis=0, keepdims=True)
    half = jnp.sum(identity * half, axis=1, keepdims=True)
    shift = jnp.sum(root * half, axis=0, keepdims=True)
    transform = (float(members - 1) ** 0.5 * root + shift).astype(BF16)
    next_in(6)

    tall = 128
    repeated = jnp.dot(transform, spread[...], preferred_element_type=F32).astype(BF16)

    def expand(b, carry):
        at = lax.broadcasted_iota(jnp.int32, (tall, members), 0) + b * tall
        pick = jnp.where(
            at // rows == lax.broadcasted_iota(jnp.int32, (tall, members), 1), 1.0, 0.0
        ).astype(BF16)
        full = jnp.dot(pick, repeated, preferred_element_type=F32)
        same = (
            lax.broadcasted_iota(jnp.int32, full.shape, 0) % rows
            == lax.broadcasted_iota(jnp.int32, full.shape, 1) % rows
        )
        weights[pl.ds(pl.multiple_of(b * tall, tall), tall), :] = jnp.where(same, full, 0.0).astype(BF16)
        return carry

    lax.fori_loop(0, members * rows // tall, expand, 0)
    lax.fori_loop(7, channels, lambda c, carry: (next_in(c), carry)[1], 0)
    own_in(1, channels - 1, 1).wait()

    high = 256

    def analyse(p, carry):
        for h in range(2):
            c = 2 * p + h
            if h == 0:
                @pl.when(p > 0)
                def _():
                    drain(arrived.at[others, pl.ds(c, 1)], in_recv.at[c])
            else:
                drain(arrived.at[others, pl.ds(c, 1)], in_recv.at[c])
            total = jnp.zeros((rows, cols), F32)
            for k in range(0, members, step):
                total = total + jnp.sum(arrived[k : k + step, c].astype(F32), axis=0)
            mean = total * (1.0 / members)
            means[h] = mean
            for k in range(0, members, step):
                part = (arrived[k : k + step, c].astype(F32) - mean[None]).astype(BF16)
                perts[k * rows : (k + step) * rows, h * cols : (h + 1) * cols] = part.reshape(step * rows, cols)

        def mix(b, inner):
            at = pl.ds(pl.multiple_of(b * high, high), high)
            shifted = jnp.dot(weights[at, :], perts[...], preferred_element_type=F32)
            for h in range(2):
                part = shifted[:, h * cols : (h + 1) * cols].reshape(high // rows, rows, cols) + means[h][None]
                analysed[pl.ds(b * (high // rows), high // rows), 2 * p + h] = part.astype(BF16)
            return inner

        lax.fori_loop(0, members * rows // high, mix, 0)

        def one(i, inner):
            last = (p == channels // 2 - 1).astype(jnp.int32)
            fixed = jnp.where(i < 4, i + 1, jnp.where(i == 4, 0, i))
            q = jnp.where(last == 1, fixed, peer(me, n, jnp.minimum(i, n - 2)))

            @pl.when(jnp.where(last == 1, (q != me).astype(jnp.int32), (i < n - 1).astype(jnp.int32)) == 1)
            def _():
                pltpu.make_async_remote_copy(
                    src_ref=analysed.at[pl.ds(q * per, per), pl.ds(2 * p, 2)],
                    dst_ref=out.at[:, pl.ds(2 * p, 2), :, columns(me)],
                    send_sem=out_send, recv_sem=out_recv.at[jnp.where(last == 1, me, n)],
                    device_id={"mem": q}, device_id_type=MESH,
                ).start()

            return inner

        lax.fori_loop(0, n, one, 0)
        return carry

    lax.fori_loop(0, channels // 2, analyse, 0)
    own_out = pltpu.make_async_copy(analysed.at[mine], out.at[:, :, :, columns(me)], own_sem.at[2])
    own_out.start()

    drain(near, gram_send)
    for c in range(channels - 3, channels):
        drain(arrived.at[others, pl.ds(c, 1)], in_send.at[c])
    drain(analysed.at[others, pl.ds(0, channels - 2)], out_recv.at[n])
    own_out.wait()

    def term(m, c, q):
        return out[m, c, :, columns(q)].astype(F32) * (weight[c] * per_weight)

    def gather(q, carry):
        for m in range(per):
            rest = term(m, 1, q)
            for c in range(2, channels - 2):
                rest = rest + term(m, c, q)
            shared[m, :, columns(q)] = rest
        return carry

    lax.fori_loop(0, n, gather, 0)

    def restore(q):
        for m in range(per):
            z0 = out[m, 0, :, columns(q)].astype(F32)
            rest = shared[m, :, columns(q)] + (term(m, channels - 2, q) + term(m, channels - 1, q))
            out[m, 0, :, columns(q)] = (z0 * a - rest).astype(BF16)
            common = z0 - rest * g
            for c in range(1, channels):
                kept = out[m, c, :, columns(q)].astype(F32)
                out[m, c, :, columns(q)] = (kept + common * (weight[c] * per_weight)).astype(BF16)

    restore(me)

    def take(i, carry):
        q = (me + i + 1) % n
        drain(out.at[:, pl.ds(channels - 2, 2), :, columns(q)], out_recv.at[q])
        restore(q)
        return carry

    lax.fori_loop(0, n - 1, take, 0)
    drain(analysed.at[others], out_send)


def put(z, out, sem):
    per, channels, _, _ = z.shape
    half = channels // 2
    copies = [
        pltpu.make_async_copy(
            z.at[m, pl.ds(h * half, half)], out.at[m, pl.ds(h * half, half)], sem.at[2 * m + h]
        )
        for m in range(per)
        for h in range(2)
    ]
    for copy in copies:
        copy.start()
    for copy in copies:
        copy.wait()


def shards(state, obs_cell, obs_value, obs_rinv, obs_count, loc_blocks, chan_weight):
    per, channels, rows, width = state.shape
    n = lax.axis_size("mem")
    members, cols = per * n, width // n
    slots = obs_cell.shape[2]
    lanes = 128
    obs_shape = (slots // lanes, lanes)
    whole = pl.BlockSpec(memory_space=pl.ANY)
    dma = pltpu.SemaphoreType.DMA
    analysed = pl.pallas_call(
        kernel,
        out_shape=pltpu.VMEM(state.shape, BF16),
        in_specs=[whole] * 7,
        out_specs=pl.BlockSpec(memory_space=pltpu.VMEM),
        scratch_shapes=[
            pltpu.SMEM(chan_weight.shape, F32),
            pltpu.SMEM((1, 1), jnp.int32),
            pltpu.SMEM((1, 9), jnp.int32),
            pltpu.VMEM(state.shape, BF16),
            pltpu.VMEM(obs_shape, jnp.int32),
            pltpu.VMEM(obs_shape, F32),
            pltpu.VMEM(obs_shape, F32),
            pltpu.VMEM((per, rows, width), F32),
            pltpu.VMEM((128, rows, cols), F32),
            pltpu.VMEM((members, 128), F32),
            pltpu.VMEM((members, 128), BF16),
            pltpu.VMEM((8, members, 128), BF16),
            pltpu.VMEM((members, channels, rows, cols), BF16),
            pltpu.VMEM((members, members * rows), BF16),
            pltpu.VMEM((members * rows, members * rows), BF16),
            pltpu.VMEM((members * rows, 2 * cols), BF16),
            pltpu.VMEM((2, rows, cols), F32),
            pltpu.VMEM((members, channels, rows, cols), BF16),
            dma((3,)),
            dma((per,)),
            dma((3,)),
            dma((3,)),
            dma, dma,
            dma((channels,)),
            dma((channels,)),
            dma,
            dma((n + 1,)),
        ],
        compiler_params=pltpu.CompilerParams(
            collective_id=0, has_side_effects=True, vmem_limit_bytes=63_800_000
        ),
        name="letkf",
    )(
        chan_weight, obs_count, loc_blocks[0],
        state, obs_cell.reshape(obs_shape), obs_value.reshape(obs_shape), obs_rinv.reshape(obs_shape),
    )

    return pl.pallas_call(
        put,
        out_shape=jax.ShapeDtypeStruct(state.shape, BF16),
        in_specs=[pl.BlockSpec(memory_space=pltpu.VMEM)],
        out_specs=whole,
        scratch_shapes=[dma((2 * per,))],
        compiler_params=pltpu.CompilerParams(vmem_limit_bytes=24 * 2**20),
        name="put",
    )(analysed)


def solution(mesh):
    placed = (
        P("mem", None, "lat", None),
        P("lat", "mem", None),
        P("lat", "mem", None),
        P("lat", "mem", None),
        P("lat", "mem"),
        P("lat", "mem", None),
        P(),
    )
    return jax.shard_map(
        shards, mesh=mesh, in_specs=placed, out_specs=P("mem", None, "lat", None), check_vma=False
    )
```
